256 devices in a mesh: req: 64 (over x, z, core), tp: 4 (over y).
Axes of the slice: x: 4, y: 4, z: 8, core: 2. Of those that a mesh axis runs over, the one named last changes fastest.
Arguments:
- attn_values: bfloat16 [16384, 2048], P('req', 'tp'), may hold values from -0.5 to 0.5
- out_proj: bfloat16 [2048, 2048], P('tp'), may hold values from -0.125 to 0.125
- residual_in: bfloat16 [16384, 2048], P(('req', 'tp')), may hold values from -0.5 to 0.5
- norm_gain: bfloat16 [2048], replicated, may hold values from 0.099609375 to 1.8984375
- final_gain: bfloat16 [2048], replicated, may hold values from 0.099609375 to 1.8984375
- router: bfloat16 [2048, 8], replicated, may hold values from -0.03125 to 0.03125
- gate_weight: bfloat16 [64, 2048, 640], P('req'), may hold values from -0.125 to 0.125
- up_weight: bfloat16 [64, 2048, 640], P('req'), may hold values from -0.125 to 0.125
- down_weight: bfloat16 [64, 640, 2048], P('req'), may hold values from -2 to 2
- row_order: int32 [16384], P(('req', 'tp')), may hold values from 0 to 16383, as said below
- routes: int32 [16384, 2], P(('req', 'tp')), may hold values from 0 to 7, all different within a row; in each aligned block of 64 rows (0 to 63, 64 to 127, ...) at most 32 rows name the same one
Outputs:
- layer_out: bfloat16 [16384, 2048], P(('req', 'tp'))
The draws below stay inside these ranges and needn't reach their ends.
Inputs may be any that keep to these rules, and one draw needn't show every extreme that they name: row_order permutes each aligned block of 64 positions within itself. `routes`: in each aligned block of 64 rows (the rows of one device) a row names two different experts and no expert is named more than 32 times; in every draw some expert is named exactly 32 times in some block.
All inputs are finite; a program needn't handle non-finite values.
Results may differ from the reference program's by a relative error of at most 0.01.
Values may be sent and summed in bfloat16 or wider, within the bound.
A program may use at most 128 MiB of HBM per device.

```python
import math
import jax
import jax.numpy as jnp
import numpy as np
from jax import lax

D = 2048
HD = 2048
EXPERTS = 8
FW = 5120
TOP = 2
TOK_DEV = 64
CAP = 32
SLICE = 640
TOKENS = 16384
N_REQ = 64


def draw_row_order(key, part):
    blocks = TOKENS // TOK_DEV
    block_keys = jax.random.split(key, blocks)
    shuffled = jax.vmap(lambda sub_key: jax.random.permutation(sub_key, TOK_DEV))(block_keys)
    offsets = jnp.arange(blocks, dtype=jnp.int32)[:, None] * TOK_DEV
    return (shuffled.astype(jnp.int32) + offsets).reshape(TOKENS)


def draw_down_weight(key, part):
    factor_key = jax.random.fold_in(key, 11)
    entry_key = jax.random.fold_in(key, 12)
    factors = jnp.exp(jax.random.uniform(factor_key, (EXPERTS,), jnp.float32, 0.0, math.log(4.0)))
    owner = jnp.arange(N_REQ, dtype=jnp.int32) // (N_REQ // EXPERTS)
    block_scale = jnp.take(factors, owner)
    entries = jax.random.truncated_normal(entry_key, -3.0, 3.0, (N_REQ, SLICE, D), jnp.float32)
    return (entries * block_scale[:, None, None] * (1.0 / math.sqrt(FW))).astype(jnp.bfloat16)


def steps_of(key, dims, cuts, smallest, largest):
    def one(dim, shards_of):
        heights = jax.random.uniform(jax.random.fold_in(jax.random.fold_in(key, 6), dim), (shards_of,), jnp.float32, smallest / len(cuts), largest / len(cuts))
        return jnp.repeat(jnp.exp(heights), dims[dim] // shards_of).reshape((-1,) + (1,) * (len(dims) - dim - 1))

    level = one(*cuts[0])
    for cut in cuts[1:]:
        level = level * one(*cut)
    return level


def routed_block(own_key, own, number, rows, amount, top, reach, lean):
    ranking = jax.random.permutation(own_key, amount)
    heavy_load, common = portions_of(amount, rows * top, reach, lean, True), portions_of(amount, rows * top, reach, lean, False)
    places = jnp.arange(amount)

    def named(tallies, turn):
        used = int((tallies > 0).sum())
        fixed = max(1, used // 4)
        passed = fixed + (places - fixed + turn * (used - fixed)) % max(1, amount - fixed)
        return jnp.zeros((amount,), jnp.int32).at[ranking[jnp.where(places < fixed, places, passed)]].set(jnp.asarray(tallies, jnp.int32))

    tallies = jnp.where(number % 4 == 0, named(heavy_load, number // 4), named(common, number - number // 4 - 1))
    mixed = jax.random.permutation(jax.random.fold_in(own, 3), amount)
    donor, receiver = mixed[0:amount // 2 * 2:2], mixed[1:amount // 2 * 2:2]
    room = jnp.minimum(tallies[donor] - 1, reach - tallies[receiver]) // 2
    room = jnp.where((donor == ranking[0]) | (receiver == ranking[0]) | (tallies[receiver] == 0), 0, jnp.maximum(room, 0))
    passed = jax.random.randint(jax.random.fold_in(own, 4), (amount // 2,), 0, 1 << 20) % (room + 1)
    tallies = tallies.at[donor].add(-passed).at[receiver].add(passed)
    items = jnp.searchsorted(jnp.cumsum(tallies), jnp.arange(rows * top), side="right").astype(jnp.int32)
    table = items.reshape(top, rows).T
    table = table[jax.random.permutation(jax.random.fold_in(own, 1), rows)]
    turn = jax.random.randint(jax.random.fold_in(own, 2), (rows, 1), 0, top)
    return jnp.take_along_axis(table, (jnp.arange(top)[None, :] + turn) % top, axis=1)


def portions_of(amount, total, reach, lean, full):
    weights = [(1 << 20) // math.isqrt(standing ** lean) + 1 for standing in range(1, amount + 1)]
    largest = reach if full else min(reach, max(-(-total // amount), total * weights[0] // sum(weights)))
    least = 1 if total - largest >= amount - 1 else 0
    counts, rest = [largest] + [least] * (amount - 1), total - largest - least * (amount - 1)
    while rest > 0:
        movable = [i for i in range(1, amount) if counts[i] < largest] or [i for i in range(1, amount) if counts[i] < reach]
        pool, left = sum([weights[i] for i in movable]), rest
        for i in movable:
            addition = min(reach - counts[i], max(1, left * weights[i] // pool), rest)
            counts[i] = counts[i] + addition
            rest = rest - addition
    return np.array(counts)


def scatter_about(stream_key, extent, scale, bound, cuts=(), kind=jnp.bfloat16):
    factor_of = steps_of(stream_key, extent, cuts, -0.22, 0.18) if cuts else 1.0
    values = jax.random.normal(stream_key, extent, jnp.float32) * scale * factor_of
    return jnp.minimum(jnp.maximum(values, -bound), bound).astype(kind)


def setup_inputs(seed: int = 0) -> dict:
    arg_keys = jax.random.split(jax.random.key(seed), 12)
    attn_values = scatter_about(arg_keys[0], (TOKENS, HD), 0.08, 0.5, ((0, 64), (1, 4)))
    out_proj = scatter_about(arg_keys[1], (HD, D), HD ** -0.5, 0.125, ((0, 4),))
    residual_in = scatter_about(arg_keys[2], (TOKENS, D), 0.08, 0.5, ((0, 256),))
    norm_gain = jnp.clip(1.0 + 0.18 * jax.random.normal(arg_keys[3], (D,), jnp.float32), 0.099609375, 1.8984375).astype(jnp.bfloat16)
    final_gain = jnp.clip(1.0 + 0.18 * jax.random.normal(arg_keys[4], (D,), jnp.float32), 0.099609375, 1.8984375).astype(jnp.bfloat16)
    router = scatter_about(arg_keys[5], (D, EXPERTS), (16 * D) ** -0.5, 0.03125)
    gate_weight = scatter_about(arg_keys[6], (N_REQ, D, SLICE), D ** -0.5, 0.125, ((0, 64),))
    up_weight = scatter_about(arg_keys[7], (N_REQ, D, SLICE), D ** -0.5, 0.125, ((0, 64),))
    down_weight = draw_down_weight(jax.random.fold_in(arg_keys[11], 71), 0)
    row_order = draw_row_order(jax.random.fold_in(arg_keys[11], 71), 0)
    routes_keys = jax.random.split(jax.random.fold_in(arg_keys[10], 1), TOKENS // TOK_DEV)
    routes_turns = jax.random.permutation(jax.random.fold_in(arg_keys[10], 3), TOKENS // TOK_DEV)
    routes = jax.vmap(lambda own, number: routed_block(jax.random.fold_in(arg_keys[10], 2), own, number, TOK_DEV, EXPERTS, TOP, CAP, 2))(routes_keys, routes_turns).reshape((TOKENS, TOP))
    return dict(attn_values=attn_values, out_proj=out_proj, residual_in=residual_in, norm_gain=norm_gain, final_gain=final_gain, router=router, gate_weight=gate_weight, up_weight=up_weight, down_weight=down_weight, row_order=row_order, routes=routes)


def root_norm(values, scale_gain):
    mean_sq = lax.optimization_barrier(jnp.mean(values * values, axis=-1, keepdims=True))
    return values * lax.rsqrt(mean_sq + 1e-06) * scale_gain.astype(jnp.float32)

def reference(attn_values, out_proj, residual_in, norm_gain, final_gain, router, gate_weight, up_weight, down_weight, row_order, routes):
    holders = N_REQ // EXPERTS
    blocks = TOKENS // TOK_DEV
    attn_out = jnp.dot(attn_values, out_proj, preferred_element_type=jnp.float32)
    stream = (residual_in.astype(jnp.float32) + attn_out).astype(jnp.bfloat16)
    normed = root_norm(stream.astype(jnp.float32), norm_gain).astype(jnp.bfloat16)
    picked = jnp.take(normed, row_order, axis=0)
    kept = jnp.take(stream, row_order, axis=0).astype(jnp.float32)
    logits = jnp.dot(picked, router, preferred_element_type=jnp.float32)
    onehot = (routes[:, :, None] == jnp.arange(EXPERTS, dtype=jnp.int32)[None, None, :]).astype(jnp.int32)
    chosen = lax.optimization_barrier(jnp.sum(logits[:, None, :] * onehot.astype(jnp.float32), axis=-1))
    weight_a = jax.nn.sigmoid(chosen[:, 0] - chosen[:, 1])
    weight_b = jax.nn.sigmoid(chosen[:, 1] - chosen[:, 0])
    flat_hot = onehot.reshape(blocks, TOK_DEV * TOP, EXPERTS)
    before = jnp.cumsum(flat_hot, axis=1) - flat_hot
    slot_rank = lax.optimization_barrier(jnp.sum(before * flat_hot, axis=-1)).reshape(TOKENS, TOP)
    position = routes * CAP + slot_rank
    slot_table = (position[:, :, None] == jnp.arange(EXPERTS * CAP, dtype=jnp.int32)[None, None, :]).astype(jnp.float32)
    dispatch = lax.optimization_barrier(jnp.sum(slot_table, axis=1)).reshape(blocks, TOK_DEV, EXPERTS * CAP)
    pair_w = jnp.stack([weight_a, weight_b], axis=1)
    combine_w = lax.optimization_barrier(jnp.sum(slot_table * pair_w[:, :, None], axis=1)).reshape(blocks, TOK_DEV, EXPERTS * CAP)
    expert_in = jnp.einsum('brc,brd->bcd', dispatch, picked.reshape(blocks, TOK_DEV, D).astype(jnp.float32)).astype(jnp.bfloat16)
    expert_in = expert_in.reshape(blocks, EXPERTS, CAP, D).transpose(1, 0, 2, 3).reshape(EXPERTS, blocks * CAP, D)
    gate_full = gate_weight.reshape(EXPERTS, holders, D, SLICE).transpose(0, 2, 1, 3).reshape(EXPERTS, D, FW)
    up_full = up_weight.reshape(EXPERTS, holders, D, SLICE).transpose(0, 2, 1, 3).reshape(EXPERTS, D, FW)
    down_full = down_weight.reshape(EXPERTS, FW, D)

    def one_expert(inputs):
        rows_in, gate_part, up_part, down_part = inputs
        gate_val = jnp.dot(rows_in, gate_part, preferred_element_type=jnp.float32)
        up_val = jnp.dot(rows_in, up_part, preferred_element_type=jnp.float32)
        hidden = (jax.nn.silu(gate_val) * up_val).astype(jnp.bfloat16)
        return jnp.dot(hidden, down_part, preferred_element_type=jnp.float32)
    expert_out = lax.map(one_expert, (expert_in, gate_full, up_full, down_full))
    expert_out = expert_out.reshape(EXPERTS, blocks, CAP, D).transpose(1, 0, 2, 3).reshape(blocks, EXPERTS * CAP, D)
    moe = jnp.einsum('brc,bcd->brd', combine_w, expert_out, precision=lax.Precision.HIGHEST).reshape(TOKENS, D)
    normed_out = root_norm(kept + moe, final_gain).astype(jnp.bfloat16)
    return jnp.zeros((TOKENS, D), jnp.bfloat16).at[row_order].set(normed_out)
```

```python
import jax
import jax.numpy as jnp
from jax import lax
from jax.sharding import Mesh, PartitionSpec as P

TOP = 2
CAP = 32
X, Z, C = 4, 8, 2
META = 128


def root_norm(values, scale_gain):
    mean_sq = jnp.mean(values * values, axis=-1, keepdims=True)
    return values * lax.rsqrt(mean_sq + 1e-06) * scale_gain.astype(jnp.float32)


def shards(
    attn_values,
    out_proj,
    residual_in,
    norm_gain,
    final_gain,
    router,
    gate_weight,
    up_weight,
    down_weight,
    row_order,
    routes,
):
    rows, width = residual_in.shape
    experts = router.shape[1]
    f32, bf16 = jnp.float32, jnp.bfloat16
    half = lax.axis_index("z") // (Z // 2)

    swap = [(0, 1), (1, 0)]
    gates = [gate_weight[0], lax.ppermute(gate_weight, "c", swap)[0]]
    ups = [up_weight[0], lax.ppermute(up_weight, "c", swap)[0]]
    downs = [down_weight[0], lax.ppermute(down_weight, "c", swap)[0]]

    attn_out = lax.psum_scatter(
        jnp.dot(attn_values, out_proj, preferred_element_type=f32).astype(bf16),
        "tp",
        scatter_dimension=0,
        tiled=True,
    ).astype(f32)
    stream = (residual_in.astype(f32) + attn_out).astype(bf16)
    normed = root_norm(stream.astype(f32), norm_gain).astype(bf16)

    local_order = lax.rem(row_order, rows)
    pick = (local_order[:, None] == jnp.arange(rows, dtype=jnp.int32)[None, :]).astype(bf16)
    picked = jnp.dot(pick, normed, preferred_element_type=f32).astype(bf16)

    logits = jnp.dot(picked, router, preferred_element_type=f32)
    onehot = (routes[:, :, None] == jnp.arange(experts, dtype=jnp.int32)).astype(jnp.int32)
    chosen = jnp.sum(logits[:, None, :] * onehot.astype(f32), axis=-1)
    weight_a = jax.nn.sigmoid(chosen[:, 0] - chosen[:, 1])
    weight_b = jax.nn.sigmoid(chosen[:, 1] - chosen[:, 0])
    flat_hot = onehot.reshape(rows * TOP, experts)
    earlier = jnp.tri(rows * TOP, k=-1, dtype=bf16)
    before = jnp.dot(earlier, flat_hot.astype(bf16), preferred_element_type=f32)
    rank = jnp.sum(before * flat_hot.astype(f32), axis=-1).reshape(rows, TOP)
    slot = (routes % 2 * (experts // 2 * CAP) + routes // 2 * CAP).astype(f32) + rank
    pair_w = jnp.stack([weight_a, weight_b], axis=1)
    w_hi = pair_w.astype(bf16)
    w_lo = (pair_w - w_hi.astype(f32)).astype(bf16)
    meta = jnp.concatenate([slot.astype(bf16), w_hi, w_lo], axis=1)
    meta = jnp.pad(meta, ((0, 0), (0, META - meta.shape[1])))

    column = lax.all_gather(jnp.concatenate([picked, meta], axis=1), "z", axis=0)
    half_slots = X * CAP
    local = column[:, :, width : width + TOP].astype(f32) - (half * half_slots).astype(f32)
    at = jnp.arange(half_slots, dtype=f32)
    table = (local[:, :, :, None] == at).astype(bf16)
    dispatch = table[:, :, 0] + table[:, :, 1]
    w = column[:, :, width + TOP : width + 3 * TOP]
    comb_hi = table[:, :, 0] * w[:, :, 0:1] + table[:, :, 1] * w[:, :, 1:2]
    comb_lo = table[:, :, 0] * w[:, :, 2:3] + table[:, :, 1] * w[:, :, 3:4]

    slots = jnp.einsum(
        "zrs,zrd->zsd", dispatch, column[:, :, :width], preferred_element_type=f32
    ).astype(bf16)
    sent = slots.reshape(Z, X, CAP, width)
    items = lax.all_to_all(sent, "x", split_axis=1, concat_axis=1, tiled=True)
    flat = items.reshape(Z * X * CAP, width)
    total = None
    for gate, up, down in zip(gates, ups, downs):
        g = jnp.dot(flat, gate, preferred_element_type=f32)
        u = jnp.dot(flat, up, preferred_element_type=f32)
        hidden = (jax.nn.silu(g) * u).astype(bf16)
        part = jnp.dot(hidden, down, preferred_element_type=f32)
        total = part if total is None else total + part
    back = total.astype(bf16).reshape(Z, X, CAP, width)
    back = lax.all_to_all(back, "x", split_axis=1, concat_axis=1, tiled=True)
    back = back.reshape(Z, half_slots, width)
    moe = jnp.einsum("zrs,zsd->zrd", comb_hi, back, preferred_element_type=f32)
    moe = moe + jnp.einsum("zrs,zsd->zrd", comb_lo, back, preferred_element_type=f32)
    moe = lax.psum_scatter(moe.astype(bf16), "z", scatter_dimension=0, tiled=True)[0]

    kept = jnp.dot(pick, stream, preferred_element_type=f32)
    done = root_norm(kept + moe.astype(f32), final_gain).astype(bf16)
    return jnp.dot(pick.T, done, preferred_element_type=f32).astype(bf16)


def solution(mesh):
    fine = Mesh(mesh.devices.reshape(X, Z, C, -1), ("x", "z", "c", "tp"))
    req = ("x", "z", "c")
    placed = (
        P(req, "tp"),
        P("tp", None),
        P((*req, "tp"), None),
        P(),
        P(),
        P(),
        P(req, None, None),
        P(req, None, None),
        P(req, None, None),
        P((*req, "tp")),
        P((*req, "tp"), None),
    )
    return jax.shard_map(
        shards, mesh=fine, in_specs=placed, out_specs=P((*req, "tp"), None), check_vma=False
    )
```

```python
import functools

import jax
import jax.numpy as jnp
from jax import lax
from jax.experimental import pallas as pl
from jax.experimental.pallas import tpu as pltpu
from jax.sharding import Mesh, PartitionSpec as P

TOP = 2
CAP = 32
X, Z, C = 4, 8, 2
HALF = X * CAP
META = 128
MESH = pl.DeviceIdType.MESH
F32, BF16 = jnp.float32, jnp.bfloat16


def root_norm(values, gain):
    mean_sq = jnp.mean(values * values, axis=-1, keepdims=True)
    return values * lax.rsqrt(mean_sq + 1e-06) * gain.astype(F32)


def greet(peers):
    barrier = pltpu.get_barrier_semaphore()
    for peer in peers:
        pl.semaphore_signal(barrier, inc=1, device_id=peer, device_id_type=MESH)
    return lambda: pl.semaphore_wait(barrier, len(peers))


def remote(src, dst, send, recv, peer):
    copy = pltpu.make_async_remote_copy(
        src_ref=src, dst_ref=dst, send_sem=send, recv_sem=recv,
        device_id=peer, device_id_type=MESH,
    )
    copy.start()
    return copy


def x_peer(mx, d):
    return {"x": lax.rem(mx + d, X)}


def front(
    tp, attn, proj, resid, gain, router, pick, first, second, places, gate, up, down,
    items, meta, kept, gate2, up2, down2,
    part, inbox, chunk, col, slots,
    tp_send, tp_recv, z_send, z_recv, x_send, x_recv, own_sem, w_send, w_recv,
):
    mx, mz = lax.axis_index("x"), lax.axis_index("z")
    mc, mt = lax.axis_index("c"), lax.axis_index("tp")
    rows, width = resid.shape
    above, below = {"z": lax.rem(mz + 1, Z)}, {"z": lax.rem(mz + Z - 1, Z)}
    other = {"c": 1 - mc}
    mates = [{"tp": lax.rem(mt + d, tp)} for d in range(1, tp)]
    ready = greet(mates + [above, below, other] + [x_peer(mx, d) for d in range(1, X)])

    def term(t):
        block = attn[pl.ds(pl.multiple_of(t * rows, rows), rows), :]
        return jnp.dot(block, proj[...], preferred_element_type=F32)

    pending = []
    for d in range(1, tp):
        part[d - 1] = term(lax.rem(mt + d, tp)).astype(BF16)
        if d == 1:
            ready()
        pending.append(
            remote(part.at[d - 1], inbox.at[d - 1], tp_send.at[d - 1], tp_recv.at[d - 1], mates[d - 1])
        )
    swaps = [
        remote(a, b, w_send.at[i], w_recv.at[i], other)
        for i, (a, b) in enumerate(((gate, gate2), (up, up2), (down, down2)))
    ]
    total = term(mt)
    for d in range(1, tp):
        pending[d - 1].wait_recv()
        total = total + inbox[d - 1].astype(F32)
    stream = (resid[...].astype(F32) + total).astype(BF16)
    normed = root_norm(stream.astype(F32), gain[...]).astype(BF16)
    picked = jnp.dot(pick[...], normed, preferred_element_type=F32).astype(BF16)
    kept[...] = jnp.dot(pick[...], stream, preferred_element_type=F32).astype(BF16)
    logits = jnp.dot(picked, router[...], preferred_element_type=F32)
    chosen_a = jnp.sum(logits * first[...], axis=-1, keepdims=True)
    chosen_b = jnp.sum(logits * second[...], axis=-1, keepdims=True)
    lane = lax.broadcasted_iota(jnp.int32, (rows, META), 1)
    notes = places[...]
    for i, w in enumerate((jax.nn.sigmoid(chosen_a - chosen_b), jax.nn.sigmoid(chosen_b - chosen_a))):
        high = w.astype(BF16).astype(F32)
        notes = notes + jnp.where(lane == 2 + i, high, 0.0)
        notes = notes + jnp.where(lane == 4 + i, w - high, 0.0)
    chunk[:, :width] = picked
    chunk[:, width:] = notes.astype(BF16)

    offset = (mz // (Z // 2) * HALF).astype(F32)
    at = lane.astype(F32)
    exchanged = []

    def spread(order, zs, block):
        note = block[:, width:]
        meta[zs] = note
        wide = note.astype(F32)
        hit = (wide[:, 0:1] - offset == at) | (wide[:, 1:2] - offset == at)
        table = jnp.where(hit, 1.0, 0.0).astype(BF16)
        found = lax.dot_general(
            table, block[:, :width], (((0,), (0,)), ((), ())), preferred_element_type=F32
        )
        slots[zs] = found.astype(BF16).reshape(X, CAP, width)
        for d in range(1, X):
            peer = x_peer(mx, d)
            exchanged.append(
                remote(
                    slots.at[zs, peer["x"]], items.at[zs, mx],
                    x_send.at[order, d - 1], x_recv.at[order, d - 1], peer,
                )
            )
        own = pltpu.make_async_copy(slots.at[zs, mx], items.at[zs, mx], own_sem.at[order])
        own.start()
        exchanged.append(own)

    far = Z // 2
    upper, lower = slice(0, rows // 2), slice(rows // 2, rows)
    rising = [remote(chunk, col.at[mz], z_send.at[0, 0], z_recv.at[0, 0], above)]
    falling = [remote(chunk, col.at[mz], z_send.at[1, 0], z_recv.at[1, 0], below)]
    spread(0, mz, chunk)
    for k in range(1, far):
        low, high = lax.rem(mz + Z - k, Z), lax.rem(mz + k, Z)
        a, b = col.at[low], col.at[high]
        if k == far - 1:
            a, b = col.at[low, upper], col.at[high, lower]
        rising[k - 1].wait_recv()
        rising.append(remote(a, a, z_send.at[0, k], z_recv.at[0, k], above))
        falling[k - 1].wait_recv()
        falling.append(remote(b, b, z_send.at[1, k], z_recv.at[1, k], below))
        spread(2 * k - 1, low, col.at[low])
        spread(2 * k, high, col.at[high])
    last = lax.rem(mz + far, Z)
    rising[-1].wait_recv()
    falling[-1].wait_recv()
    spread(Z - 1, last, col.at[last])
    for copy in pending + rising + falling:
        copy.wait_send()
    for copy in exchanged + swaps:
        copy.wait()


def back(
    partial, meta, kept, pick, gain, out,
    got, part, inbox, x_send, x_recv, own_sem, z_send, z_recv,
):
    mx, mz = lax.axis_index("x"), lax.axis_index("z")
    rows, width = kept.shape
    greet(
        [{"z": lax.rem(mz + d, Z)} for d in range(1, Z)] + [x_peer(mx, d) for d in range(1, X)]
    )()
    far = Z // 2
    steps = [far]
    for k in range(far - 1, 0, -1):
        steps += [k, Z - k]
    steps.append(0)
    coming, going = [], []
    for o, s in enumerate(steps):
        zs = lax.rem(mz + s, Z)
        copies = []
        for d in range(1, X):
            peer = x_peer(mx, d)
            copies.append(
                remote(
                    partial.at[zs, peer["x"]], got.at[zs, mx],
                    x_send.at[o, d - 1], x_recv.at[o, d - 1], peer,
                )
            )
        own = pltpu.make_async_copy(partial.at[zs, mx], got.at[zs, mx], own_sem.at[o])
        own.start()
        coming.append((copies, own))
    offset = (mz // (Z // 2) * HALF).astype(F32)
    at = lax.broadcasted_iota(jnp.int32, (rows, HALF), 1).astype(F32)
    total = None
    for o, s in enumerate(steps):
        zs = lax.rem(mz + s, Z)
        note = meta[zs].astype(F32)
        hit_a, hit_b = note[:, 0:1] - offset == at, note[:, 1:2] - offset == at
        high = jnp.where(hit_a, note[:, 2:3], 0.0) + jnp.where(hit_b, note[:, 3:4], 0.0)
        low = jnp.where(hit_a, note[:, 4:5], 0.0) + jnp.where(hit_b, note[:, 5:6], 0.0)
        copies, own = coming[o]
        own.wait()
        for copy in copies:
            copy.wait_recv()
        block = got[zs].reshape(HALF, width)
        value = jnp.dot(high.astype(BF16), block, preferred_element_type=F32)
        value = value + jnp.dot(low.astype(BF16), block, preferred_element_type=F32)
        if s == 0:
            total = value
        else:
            part[o] = value.astype(BF16)
            going.append(
                remote(part.at[o], inbox.at[o], z_send.at[o], z_recv.at[o], {"z": zs})
            )
    for o, copy in enumerate(going):
        copy.wait_recv()
        total = total + inbox[o].astype(F32)
    done = root_norm(kept[...].astype(F32) + total, gain[...]).astype(BF16)
    out[...] = lax.dot_general(
        pick[...], done, (((0,), (0,)), ((), ())), preferred_element_type=F32
    ).astype(BF16)
    for copies, _ in coming:
        for copy in copies:
            copy.wait_send()
    for copy in going:
        copy.wait_send()


def shards(
    attn_values,
    out_proj,
    residual_in,
    norm_gain,
    final_gain,
    router,
    gate_weight,
    up_weight,
    down_weight,
    row_order,
    routes,
):
    rows, width = residual_in.shape
    experts = router.shape[1]
    tp = lax.axis_size("tp")
    shape = jax.ShapeDtypeStruct
    dma = pltpu.SemaphoreType.DMA
    vmem = pl.BlockSpec(memory_space=pltpu.VMEM)
    hbm = pl.BlockSpec(memory_space=pl.ANY)

    local_order = lax.rem(row_order, rows)
    pick = (local_order[:, None] == jnp.arange(rows, dtype=jnp.int32)[None, :]).astype(BF16)
    onehot = (routes[:, :, None] == jnp.arange(experts, dtype=jnp.int32)).astype(F32)
    flat_hot = onehot.reshape(rows * TOP, experts)
    earlier = jnp.tri(rows * TOP, k=-1, dtype=BF16)
    before = jnp.dot(earlier, flat_hot.astype(BF16), preferred_element_type=F32)
    rank = jnp.sum(before * flat_hot, axis=-1).reshape(rows, TOP)
    slot = (routes % 2 * HALF + routes // 2 * CAP).astype(F32) + rank
    places = jnp.pad(slot, ((0, 0), (0, META - TOP)))
    wide = ((0, 0), (0, META - experts))
    first, second = jnp.pad(onehot[:, 0], wide), jnp.pad(onehot[:, 1], wide)

    items, meta, kept, gate2, up2, down2 = pl.pallas_call(
        functools.partial(front, tp),
        out_shape=(
            shape((Z, X, CAP, width), BF16),
            shape((Z, rows, META), BF16),
            shape((rows, width), BF16),
            shape(gate_weight.shape[1:], BF16),
            shape(up_weight.shape[1:], BF16),
            shape(down_weight.shape[1:], BF16),
        ),
        in_specs=[vmem] * 9 + [hbm] * 3,
        out_specs=(vmem, vmem, vmem, hbm, hbm, hbm),
        scratch_shapes=[
            pltpu.VMEM((tp - 1, rows, width), BF16),
            pltpu.VMEM((tp - 1, rows, width), BF16),
            pltpu.VMEM((rows, width + META), BF16),
            pltpu.VMEM((Z, rows, width + META), BF16),
            pltpu.VMEM((Z, X, CAP, width), BF16),
            dma((tp - 1,)), dma((tp - 1,)),
            dma((2, Z // 2)), dma((2, Z // 2)),
            dma((Z, X - 1)), dma((Z, X - 1)),
            dma((Z,)), dma((3,)), dma((3,)),
        ],
        compiler_params=pltpu.CompilerParams(
            collective_id=0, has_side_effects=True, vmem_limit_bytes=40 << 20
        ),
        name="front",
    )(
        attn_values, out_proj, residual_in, norm_gain[None], jnp.pad(router, wide), pick,
        first, second, places, gate_weight[0], up_weight[0], down_weight[0],
    )

    flat = items.reshape(Z * X * CAP, width)
    total = None
    for gate, up, down in (
        (gate_weight[0], up_weight[0], down_weight[0]), (gate2, up2, down2)
    ):
        g = jnp.dot(flat, gate, preferred_element_type=F32)
        u = jnp.dot(flat, up, preferred_element_type=F32)
        hidden = (jax.nn.silu(g) * u).astype(BF16)
        value = jnp.dot(hidden, down, preferred_element_type=F32)
        total = value if total is None else total + value

    return pl.pallas_call(
        back,
        out_shape=shape((rows, width), BF16),
        in_specs=[vmem] * 5,
        out_specs=vmem,
        scratch_shapes=[
            pltpu.VMEM((Z, X, CAP, width), BF16),
            pltpu.VMEM((Z - 1, rows, width), BF16),
            pltpu.VMEM((Z - 1, rows, width), BF16),
            dma((Z, X - 1)), dma((Z, X - 1)), dma((Z,)),
            dma((Z - 1,)), dma((Z - 1,)),
        ],
        compiler_params=pltpu.CompilerParams(
            collective_id=1, has_side_effects=True, vmem_limit_bytes=40 << 20
        ),
        name="back",
    )(total.astype(BF16).reshape(Z, X, CAP, width), meta, kept, pick, final_gain[None])


def solution(mesh):
    fine = Mesh(mesh.devices.reshape(X, Z, C, -1), ("x", "z", "c", "tp"))
    req = ("x", "z", "c")
    placed = (
        P(req, "tp"),
        P("tp", None),
        P((*req, "tp"), None),
        P(),
        P(),
        P(),
        P(req, None, None),
        P(req, None, None),
        P(req, None, None),
        P((*req, "tp")),
        P((*req, "tp"), None),
    )
    return jax.shard_map(
        shards, mesh=fine, in_specs=placed, out_specs=P((*req, "tp"), None), check_vma=False
    )
```

```python
import functools

import jax
import jax.numpy as jnp
from jax import lax
from jax.experimental import pallas as pl
from jax.experimental.pallas import tpu as pltpu
from jax.sharding import Mesh, PartitionSpec as P

TOP = 2
CAP = 32
X, Z, C = 4, 8, 2
HALF = X * CAP
META = 128
MESH = pl.DeviceIdType.MESH
F32, BF16 = jnp.float32, jnp.bfloat16


def root_norm(values, gain):
    mean_sq = jnp.mean(values * values, axis=-1, keepdims=True)
    return values * lax.rsqrt(mean_sq + 1e-06) * gain.astype(F32)


def greet(peers):
    barrier = pltpu.get_barrier_semaphore()
    for peer in peers:
        pl.semaphore_signal(barrier, inc=1, device_id=peer, device_id_type=MESH)
    return lambda: pl.semaphore_wait(barrier, len(peers))


def remote(src, dst, send, recv, peer):
    copy = pltpu.make_async_remote_copy(
        src_ref=src, dst_ref=dst, send_sem=send, recv_sem=recv,
        device_id=peer, device_id_type=MESH,
    )
    copy.start()
    return copy


def x_peer(mx, d):
    return {"x": lax.rem(mx + d, X)}


PLACES = (0, -1, -3, 3, 4, -2, 1, 2)


def layer(
    tp, attn, proj, resid, gain, last_gain, router, order, routes, gate, up, down,
    out,
    part, inbox, chunk, col, slots, items, partial, got, tail, tails, hidden,
    gates, ups, downs,
    tp_send, tp_recv, z_send, z_recv, x_send, x_recv, own_sem,
    r_send, r_recv, r_own, t_send, t_recv, w_own, w_send, w_recv,
):
    mx, mz = lax.axis_index("x"), lax.axis_index("z")
    mc, mt = lax.axis_index("c"), lax.axis_index("tp")
    rows, width = resid.shape
    units = gate.shape[1]
    above, below = {"z": lax.rem(mz + 1, Z)}, {"z": lax.rem(mz + Z - 1, Z)}
    other = {"c": 1 - mc}
    mates = [{"tp": lax.rem(mt + d, tp)} for d in range(1, tp)]
    column = [{"z": lax.rem(mz + d, Z)} for d in range(1, Z)]
    ready = greet(mates + column + [other] + [x_peer(mx, d) for d in range(1, X)])

    loads = []
    near, far_side = pl.ds(0, units), pl.ds(units, units)
    for i, (a, b) in enumerate(
        ((gate, gates.at[:, near]), (up, ups.at[:, near]), (down, downs.at[near, :]))
    ):
        copy = pltpu.make_async_copy(a, b, w_own.at[i])
        copy.start()
        loads.append(copy)

    def term(t):
        block = attn[pl.ds(pl.multiple_of(t * rows, rows), rows), :]
        return jnp.dot(block, proj[...], preferred_element_type=F32)

    pending = []
    for d in range(1, tp):
        part[d - 1] = term(lax.rem(mt + d, tp)).astype(BF16)
        if d == 1:
            ready()
        pending.append(
            remote(part.at[d - 1], inbox.at[d - 1], tp_send.at[d - 1], tp_recv.at[d - 1], mates[d - 1])
        )
    swaps = [
        remote(a, b, w_send.at[i], w_recv.at[i], other)
        for i, (a, b) in enumerate(
            ((gate, gates.at[:, far_side]), (up, ups.at[:, far_side]), (down, downs.at[far_side, :]))
        )
    ]
    total = term(mt)

    down_rows = lax.broadcasted_iota(jnp.int32, (rows, rows), 0)
    along = lax.broadcasted_iota(jnp.int32, (rows, rows), 1)
    upright = lambda v: jnp.sum(
        jnp.where(down_rows == along, v.astype(F32), 0.0), axis=1, keepdims=True
    )
    pick_t = jnp.where((order[...] & (rows - 1)) == down_rows, 1.0, 0.0).astype(BF16)
    earlier = jnp.where(along < down_rows, 1.0, 0.0).astype(BF16)
    route = routes[...]
    names = lax.broadcasted_iota(jnp.int32, (rows, router.shape[0]), 1).astype(F32)
    hot = [jnp.where(upright(route[k : k + 1, :]) == names, 1.0, 0.0) for k in range(TOP)]
    before = jnp.dot(earlier, (hot[0] + hot[1]).astype(BF16), preferred_element_type=F32)
    base = (route & 1) * HALF + (route >> 1) * CAP
    lane = lax.broadcasted_iota(jnp.int32, (rows, META), 1)
    notes = jnp.zeros((rows, META), F32)
    for k in range(TOP):
        rank = jnp.sum(before * hot[k], axis=1, keepdims=True)
        notes = notes + jnp.where(lane == k, upright(base[k : k + 1, :]) + rank, 0.0)

    for d in range(1, tp):
        pending[d - 1].wait_recv()
        total = total + inbox[d - 1].astype(F32)
    stream = (resid[...].astype(F32) + total).astype(BF16)
    normed = root_norm(stream.astype(F32), gain[...]).astype(BF16)
    across = (((0,), (0,)), ((), ()))
    picked = lax.dot_general(pick_t, normed, across, preferred_element_type=F32).astype(BF16)
    logits = lax.dot_general(
        picked, router[...], (((1,), (1,)), ((), ())), preferred_element_type=F32
    )
    chosen = [jnp.sum(logits * hot[k], axis=1, keepdims=True) for k in range(TOP)]
    for k in range(TOP):
        w = jax.nn.sigmoid(chosen[k] - chosen[1 - k])
        high = w.astype(BF16).astype(F32)
        notes = notes + jnp.where(lane == 2 + k, high, 0.0)
        notes = notes + jnp.where(lane == 4 + k, w - high, 0.0)
    chunk[:, :width] = picked
    chunk[:, width:] = notes.astype(BF16)

    offset = (mz // (Z // 2) * HALF).astype(F32)
    at = lane.astype(F32)
    sent = {}

    def block_of(p):
        s = PLACES[p]
        return chunk if s == 0 else col.at[lax.rem(mz + s + Z, Z)]

    def spread(p):
        block = block_of(p)
        wide = block[:, width:].astype(F32)
        hit = (wide[:, 0:1] - offset == at) | (wide[:, 1:2] - offset == at)
        table = jnp.where(hit, 1.0, 0.0).astype(BF16)
        found = lax.dot_general(table, block[:, :width], across, preferred_element_type=F32)
        slots[p] = found.astype(BF16).reshape(X, CAP, width)
        copies = []
        for d in range(1, X):
            peer = x_peer(mx, d)
            copies.append(
                remote(
                    slots.at[p, peer["x"]], items.at[p, mx],
                    x_send.at[p, d - 1], x_recv.at[p, d - 1], peer,
                )
            )
        own = pltpu.make_async_copy(slots.at[p, mx], items.at[p, mx], own_sem.at[p])
        own.start()
        sent[p] = copies, own

    far = Z // 2
    upper, lower = slice(0, rows // 2), slice(rows // 2, rows)
    rising = [remote(chunk, col.at[mz], z_send.at[0, 0], z_recv.at[0, 0], above)]
    falling = [remote(chunk, col.at[mz], z_send.at[1, 0], z_recv.at[1, 0], below)]
    spread(0)
    soon = {1: (1, 6), 2: (5,), 3: (2, 3)}
    for k in range(1, far):
        low, high = lax.rem(mz + Z - k, Z), lax.rem(mz + k, Z)
        a, b = col.at[low], col.at[high]
        if k == far - 1:
            a, b = col.at[low, upper], col.at[high, lower]
        rising[k - 1].wait_recv()
        rising.append(remote(a, a, z_send.at[0, k], z_recv.at[0, k], above))
        falling[k - 1].wait_recv()
        falling.append(remote(b, b, z_send.at[1, k], z_recv.at[1, k], below))
        for p in soon[k]:
            spread(p)
    rising[-1].wait_recv()
    falling[-1].wait_recv()
    spread(4)
    spread(7)

    for copy in loads:
        copy.wait()
    for copy in swaps:
        copy.wait_recv()

    tile = 256

    def experts(first):
        for p in (first, first + 1):
            copies, own = sent[p]
            own.wait()
            for copy in copies:
                copy.wait_recv()

        @pl.loop(0, 2 * units // tile)
        def _(j):
            at_j = pl.ds(pl.multiple_of(j * tile, tile), tile)
            flat = items[first : first + 2].reshape(2 * HALF, width)
            g = jnp.dot(flat, gates[:, at_j], preferred_element_type=F32)
            u = jnp.dot(flat, ups[:, at_j], preferred_element_type=F32)
            hidden[:, at_j] = (g / (1.0 + jnp.exp(-g)) * u).astype(BF16)

        @pl.loop(0, width // tile)
        def _(j):
            at_j = pl.ds(pl.multiple_of(j * tile, tile), tile)
            value = jnp.dot(hidden[...], downs[:, at_j], preferred_element_type=F32)
            partial[first : first + 2, :, :, at_j] = value.astype(BF16).reshape(2, X, CAP, tile)

    returned = {}

    def give_back(p):
        copies = []
        for d in range(1, X):
            peer = x_peer(mx, d)
            copies.append(
                remote(
                    partial.at[p, peer["x"]], got.at[p, mx],
                    r_send.at[p, d - 1], r_recv.at[p, d - 1], peer,
                )
            )
        own = pltpu.make_async_copy(partial.at[p, mx], got.at[p, mx], r_own.at[p])
        own.start()
        returned[p] = copies, own

    going = []

    def combine(p):
        note = block_of(p)[:, width:].astype(F32)
        hit_a, hit_b = note[:, 0:1] - offset == at, note[:, 1:2] - offset == at
        high = jnp.where(hit_a, note[:, 2:3], 0.0) + jnp.where(hit_b, note[:, 3:4], 0.0)
        low = jnp.where(hit_a, note[:, 4:5], 0.0) + jnp.where(hit_b, note[:, 5:6], 0.0)
        copies, own = returned[p]
        own.wait()
        for copy in copies:
            copy.wait_recv()
        block = got[p].reshape(HALF, width)
        value = jnp.dot(high.astype(BF16), block, preferred_element_type=F32)
        value = value + jnp.dot(low.astype(BF16), block, preferred_element_type=F32)
        if p == 0:
            return value
        tail[p - 1] = value.astype(BF16)
        peer = {"z": lax.rem(mz + PLACES[p] + Z, Z)}
        going.append(
            remote(tail.at[p - 1], tails.at[p - 1], t_send.at[p - 1], t_recv.at[p - 1], peer)
        )

    experts(0)
    experts(2)
    give_back(2)
    give_back(3)
    experts(4)
    give_back(4)
    give_back(5)
    combine(2)
    combine(3)
    experts(6)
    for p in (7, 6, 1, 0):
        give_back(p)
    for p in (4, 5, 7, 6, 1):
        combine(p)
    total = combine(0)
    for i, copy in enumerate(going):
        copy.wait_recv()
    for i in range(Z - 1):
        total = total + tails[i].astype(F32)
    kept = lax.dot_general(pick_t, stream, across, preferred_element_type=F32)
    done = root_norm(kept + total, last_gain[...]).astype(BF16)
    out[...] = jnp.dot(pick_t, done, preferred_element_type=F32).astype(BF16)
    for copy in pending + rising + falling + swaps + going:
        copy.wait_send()
    for group in (sent, returned):
        for copies, _ in group.values():
            for copy in copies:
                copy.wait_send()


def shards(
    attn_values,
    out_proj,
    residual_in,
    norm_gain,
    final_gain,
    router,
    gate_weight,
    up_weight,
    down_weight,
    row_order,
    routes,
):
    rows, width = residual_in.shape
    units = gate_weight.shape[-1]
    tp = lax.axis_size("tp")
    dma = pltpu.SemaphoreType.DMA
    vmem = pl.BlockSpec(memory_space=pltpu.VMEM)
    hbm = pl.BlockSpec(memory_space=pl.ANY)
    block = pltpu.VMEM((Z, X, CAP, width), BF16)
    return pl.pallas_call(
        functools.partial(layer, tp),
        out_shape=jax.ShapeDtypeStruct((rows, width), BF16),
        in_specs=[vmem] * 8 + [hbm] * 3,
        out_specs=vmem,
        scratch_shapes=[
            pltpu.VMEM((tp - 1, rows, width), BF16),
            pltpu.VMEM((tp - 1, rows, width), BF16),
            pltpu.VMEM((rows, width + META), BF16),
            pltpu.VMEM((Z, rows, width + META), BF16),
            block, block, block, block,
            pltpu.VMEM((Z - 1, rows, width), BF16),
            pltpu.VMEM((Z - 1, rows, width), BF16),
            pltpu.VMEM((2 * HALF, 2 * units), BF16),
            pltpu.VMEM((width, 2 * units), BF16),
            pltpu.VMEM((width, 2 * units), BF16),
            pltpu.VMEM((2 * units, width), BF16),
            dma((tp - 1,)), dma((tp - 1,)),
            dma((2, Z // 2)), dma((2, Z // 2)),
            dma((Z, X - 1)), dma((Z, X - 1)), dma((Z,)),
            dma((Z, X - 1)), dma((Z, X - 1)), dma((Z,)),
            dma((Z - 1,)), dma((Z - 1,)),
            dma((3,)), dma((3,)), dma((3,)),
        ],
        compiler_params=pltpu.CompilerParams(
            collective_id=0, has_side_effects=True, vmem_limit_bytes=58 << 20
        ),
        name="layer",
    )(
        attn_values, out_proj, residual_in, norm_gain[None], final_gain[None], router.T,
        row_order[None], routes.T, gate_weight[0], up_weight[0], down_weight[0],
    )


def solution(mesh):
    fine = Mesh(mesh.devices.reshape(X, Z, C, -1), ("x", "z", "c", "tp"))
    req = ("x", "z", "c")
    placed = (
        P(req, "tp"),
        P("tp", None),
        P((*req, "tp"), None),
        P(),
        P(),
        P(),
        P(req, None, None),
        P(req, None, None),
        P(req, None, None),
        P((*req, "tp")),
        P((*req, "tp"), None),
    )
    return jax.shard_map(
        shards, mesh=fine, in_specs=placed, out_specs=P((*req, "tp"), None), check_vma=False
    )
```

```python
import functools

import jax
import jax.numpy as jnp
from jax import lax
from jax.experimental import pallas as pl
from jax.experimental.pallas import tpu as pltpu
from jax.sharding import Mesh, PartitionSpec as P

TOP = 2
CAP = 32
X, Z, C = 4, 8, 2
HALF = X * CAP
META = 128
MESH = pl.DeviceIdType.MESH
F32, BF16 = jnp.float32, jnp.bfloat16


def root_norm(values, gain):
    mean_sq = jnp.mean(values * values, axis=-1, keepdims=True)
    return values * lax.rsqrt(mean_sq + 1e-06) * gain.astype(F32)


def greet(peers):
    barrier = pltpu.get_barrier_semaphore()
    for peer in peers:
        pl.semaphore_signal(barrier, inc=1, device_id=peer, device_id_type=MESH)
    return lambda: pl.semaphore_wait(barrier, len(peers))


def remote(src, dst, send, recv, peer):
    copy = pltpu.make_async_remote_copy(
        src_ref=src, dst_ref=dst, send_sem=send, recv_sem=recv,
        device_id=peer, device_id_type=MESH,
    )
    copy.start()
    return copy


def x_peer(mx, d):
    return {"x": lax.rem(mx + d, X)}


PLACES = (0, -1, -3, 3, 4, -2, 1, 2)


def layer(
    tp, attn, proj, resid, gain, last_gain, router, order, routes, gate, up, down,
    out,
    values, weights, residual, part, inbox, chunk, col, slots, items, partial, got,
    tail, tails, hidden, gates, ups, downs, in_sem,
    tp_send, tp_recv, z_send, z_recv, x_send, x_recv, own_sem,
    r_send, r_recv, r_own, t_send, t_recv, w_own, w_send, w_recv,
):
    mx, mz = lax.axis_index("x"), lax.axis_index("z")
    mc, mt = lax.axis_index("c"), lax.axis_index("tp")
    rows, width = resid.shape
    units = gate.shape[1]
    above, below = {"z": lax.rem(mz + 1, Z)}, {"z": lax.rem(mz + Z - 1, Z)}
    other = {"c": 1 - mc}
    mates = [{"tp": lax.rem(mt + d, tp)} for d in range(1, tp)]
    ready = greet(mates + [above, below, other] + [x_peer(mx, d) for d in range(1, X)])

    first_loads = []
    for i, (a, b) in enumerate(((attn, values), (proj, weights), (resid, residual))):
        copy = pltpu.make_async_copy(a, b, in_sem.at[i])
        copy.start()
        first_loads.append(copy)
    loads = []
    near, far_side = pl.ds(0, units), pl.ds(units, units)
    for i, (a, b) in enumerate(
        ((gate, gates.at[:, near]), (up, ups.at[:, near]), (down, downs.at[near, :]))
    ):
        copy = pltpu.make_async_copy(a, b, w_own.at[i])
        copy.start()
        loads.append(copy)

    def term(t):
        block = values[pl.ds(pl.multiple_of(t * rows, rows), rows), :]
        return jnp.dot(block, weights[...], preferred_element_type=F32)

    for copy in first_loads:
        copy.wait()
    pending = []
    turns = sorted(range(1, tp), key=lambda d: -min(d, tp - d))
    for d in turns:
        part[d - 1] = term(lax.rem(mt + d, tp)).astype(BF16)
        if not pending:
            ready()
        pending.append(
            remote(part.at[d - 1], inbox.at[d - 1], tp_send.at[d - 1], tp_recv.at[d - 1], mates[d - 1])
        )
    swaps = [
        remote(a, b, w_send.at[i], w_recv.at[i], other)
        for i, (a, b) in enumerate(
            ((gate, gates.at[:, far_side]), (up, ups.at[:, far_side]), (down, downs.at[far_side, :]))
        )
    ]
    total = term(mt)

    down_rows = lax.broadcasted_iota(jnp.int32, (rows, rows), 0)
    along = lax.broadcasted_iota(jnp.int32, (rows, rows), 1)
    upright = lambda v: jnp.sum(
        jnp.where(down_rows == along, v.astype(F32), 0.0), axis=1, keepdims=True
    )
    pick_t = jnp.where((order[...] & (rows - 1)) == down_rows, 1.0, 0.0).astype(BF16)
    earlier = jnp.where(along < down_rows, 1.0, 0.0).astype(BF16)
    route = routes[...]
    names = lax.broadcasted_iota(jnp.int32, (rows, router.shape[0]), 1).astype(F32)
    hot = [jnp.where(upright(route[k : k + 1, :]) == names, 1.0, 0.0) for k in range(TOP)]
    before = jnp.dot(earlier, (hot[0] + hot[1]).astype(BF16), preferred_element_type=F32)
    base = (route & 1) * HALF + (route >> 1) * CAP
    lane = lax.broadcasted_iota(jnp.int32, (rows, META), 1)
    notes = jnp.zeros((rows, META), F32)
    for k in range(TOP):
        rank = jnp.sum(before * hot[k], axis=1, keepdims=True)
        notes = notes + jnp.where(lane == k, upright(base[k : k + 1, :]) + rank, 0.0)
    notes = jnp.dot(pick_t, notes.astype(BF16), preferred_element_type=F32)
    hot = [jnp.dot(pick_t, h.astype(BF16), preferred_element_type=F32) for h in hot]

    for copy, d in zip(pending, turns):
        copy.wait_recv()
        total = total + inbox[d - 1].astype(F32)
    stream = (residual[...].astype(F32) + total).astype(BF16)
    normed = root_norm(stream.astype(F32), gain[...].astype(F32).reshape(1, width)).astype(BF16)
    across = (((0,), (0,)), ((), ()))
    logits = lax.dot_general(
        normed, router[...], (((1,), (1,)), ((), ())), preferred_element_type=F32
    )
    chosen = [jnp.sum(logits * hot[k], axis=1, keepdims=True) for k in range(TOP)]
    for k in range(TOP):
        w = jax.nn.sigmoid(chosen[k] - chosen[1 - k])
        high = w.astype(BF16).astype(F32)
        notes = notes + jnp.where(lane == 2 + k, high, 0.0)
        notes = notes + jnp.where(lane == 4 + k, w - high, 0.0)
    chunk[:, :width] = normed
    chunk[:, width:] = notes.astype(BF16)

    offset = (mz // (Z // 2) * HALF).astype(F32)
    at = lane.astype(F32)
    sent = {}

    def block_of(p):
        s = PLACES[p]
        return chunk if s == 0 else col.at[lax.rem(mz + s + Z, Z)]

    def spread(p):
        block = block_of(p)
        wide = block[:, width:].astype(F32)
        hit = (wide[:, 0:1] - offset == at) | (wide[:, 1:2] - offset == at)
        table = jnp.where(hit, 1.0, 0.0).astype(BF16)
        found = lax.dot_general(table, block[:, :width], across, preferred_element_type=F32)
        slots[p] = found.astype(BF16).reshape(X, CAP, width)
        copies = []
        for d in range(1, X):
            peer = x_peer(mx, d)
            copies.append(
                remote(
                    slots.at[p, peer["x"]], items.at[p, mx],
                    x_send.at[p, d - 1], x_recv.at[p, d - 1], peer,
                )
            )
        own = pltpu.make_async_copy(slots.at[p, mx], items.at[p, mx], own_sem.at[p])
        own.start()
        sent[p] = copies, own

    far = Z // 2
    upper, lower = slice(0, rows // 2), slice(rows // 2, rows)
    rising = [remote(chunk, col.at[mz], z_send.at[0, 0], z_recv.at[0, 0], above)]
    falling = [remote(chunk, col.at[mz], z_send.at[1, 0], z_recv.at[1, 0], below)]
    spread(0)
    soon = {1: (1, 6), 2: (), 3: (2, 3)}
    for k in range(1, far):
        low, high = lax.rem(mz + Z - k, Z), lax.rem(mz + k, Z)
        a, b = col.at[low], col.at[high]
        if k == far - 1:
            a, b = col.at[low, upper], col.at[high, lower]
        rising[k - 1].wait_recv()
        rising.append(remote(a, a, z_send.at[0, k], z_recv.at[0, k], above))
        falling[k - 1].wait_recv()
        falling.append(remote(b, b, z_send.at[1, k], z_recv.at[1, k], below))
        for p in soon[k]:
            spread(p)
    rising[-1].wait_recv()
    falling[-1].wait_recv()
    spread(4)
    spread(5)
    spread(7)

    for copy in loads:
        copy.wait()
    for copy in swaps:
        copy.wait_recv()

    tile = 256

    def experts(first):
        for p in (first, first + 1):
            copies, own = sent[p]
            own.wait()
            for copy in copies:
                copy.wait_recv()

        @pl.loop(0, 2 * units // tile)
        def _(j):
            at_j = pl.ds(pl.multiple_of(j * tile, tile), tile)
            flat = items[first : first + 2].reshape(2 * HALF, width)
            g = jnp.dot(flat, gates[:, at_j], preferred_element_type=F32)
            u = jnp.dot(flat, ups[:, at_j], preferred_element_type=F32)
            hidden[:, at_j] = (g / (1.0 + jnp.exp(-g)) * u).astype(BF16)

        @pl.loop(0, width // tile)
        def _(j):
            at_j = pl.ds(pl.multiple_of(j * tile, tile), tile)
            value = jnp.dot(hidden[...], downs[:, at_j], preferred_element_type=F32)
            partial[first : first + 2, :, :, at_j] = value.astype(BF16).reshape(2, X, CAP, tile)

    returned = {}

    def give_back(p):
        copies = []
        for d in range(1, X):
            peer = x_peer(mx, d)
            copies.append(
                remote(
                    partial.at[p, peer["x"]], got.at[p, mx],
                    r_send.at[p, d - 1], r_recv.at[p, d - 1], peer,
                )
            )
        own = pltpu.make_async_copy(partial.at[p, mx], got.at[p, mx], r_own.at[p])
        own.start()
        returned[p] = copies, own

    def combine(p):
        note = block_of(p)[:, width:].astype(F32)
        hit_a, hit_b = note[:, 0:1] - offset == at, note[:, 1:2] - offset == at
        high = jnp.where(hit_a, note[:, 2:3], 0.0) + jnp.where(hit_b, note[:, 3:4], 0.0)
        low = jnp.where(hit_a, note[:, 4:5], 0.0) + jnp.where(hit_b, note[:, 5:6], 0.0)
        copies, own = returned[p]
        own.wait()
        for copy in copies:
            copy.wait_recv()
        block = got[p].reshape(HALF, width)
        value = jnp.dot(high.astype(BF16), block, preferred_element_type=F32)
        return value + jnp.dot(low.astype(BF16), block, preferred_element_type=F32)

    sums = ([], [])

    def pass_on(way, k, value):
        if k == 0:
            kept_rows = (upper, lower)[way]
            tail[way, k, kept_rows] = value[kept_rows].astype(BF16)
            a, b = tail.at[way, k, kept_rows], tails.at[way, k, kept_rows]
        else:
            sums[way][k - 1].wait_recv()
            if k == 1:
                kept_rows = (upper, lower)[way]
                rest = (lower, upper)[way]
                added = value[kept_rows] + tails[way, 0, kept_rows].astype(F32)
                tail[way, k, kept_rows] = added.astype(BF16)
                tail[way, k, rest] = value[rest].astype(BF16)
            else:
                tail[way, k] = (value + tails[way, k - 1].astype(F32)).astype(BF16)
            a, b = tail.at[way, k], tails.at[way, k]
        sums[way].append(
            remote(a, b, t_send.at[way, k], t_recv.at[way, k], (above, below)[way])
        )

    experts(0)
    experts(2)
    give_back(2)
    give_back(3)
    experts(4)
    give_back(4)
    give_back(5)
    experts(6)
    for p in (7, 6, 1, 0):
        give_back(p)
    ahead, behind = combine(3), combine(2)
    value = combine(4)
    pass_on(0, 0, value)
    pass_on(1, 0, value)
    pass_on(0, 1, ahead)
    pass_on(1, 1, behind)
    behind, ahead = combine(5), combine(7)
    pass_on(0, 2, ahead)
    pass_on(1, 2, behind)
    ahead, behind = combine(6), combine(1)
    pass_on(0, 3, ahead)
    pass_on(1, 3, behind)
    total = combine(0)
    for way in (0, 1):
        sums[way][far - 1].wait_recv()
        total = total + tails[way, far - 1].astype(F32)
    last = last_gain[...].astype(F32).reshape(1, width)
    out[...] = root_norm(stream.astype(F32) + total, last).astype(BF16)
    for copy in pending + rising + falling + swaps + sums[0] + sums[1]:
        copy.wait_send()
    for group in (sent, returned):
        for copies, _ in group.values():
            for copy in copies:
                copy.wait_send()


def shards(
    attn_values,
    out_proj,
    residual_in,
    norm_gain,
    final_gain,
    router,
    gate_weight,
    up_weight,
    down_weight,
    row_order,
    routes,
):
    rows, width = residual_in.shape
    units = gate_weight.shape[-1]
    tp = lax.axis_size("tp")
    dma = pltpu.SemaphoreType.DMA
    vmem = pl.BlockSpec(memory_space=pltpu.VMEM)
    hbm = pl.BlockSpec(memory_space=pl.ANY)
    block = pltpu.VMEM((Z, X, CAP, width), BF16)
    return pl.pallas_call(
        functools.partial(layer, tp),
        out_shape=jax.ShapeDtypeStruct((rows, width), BF16),
        in_specs=[hbm] * 3 + [vmem] * 5 + [hbm] * 3,
        out_specs=vmem,
        scratch_shapes=[
            pltpu.VMEM(attn_values.shape, BF16),
            pltpu.VMEM(out_proj.shape, BF16),
            pltpu.VMEM((rows, width), BF16),
            pltpu.VMEM((tp - 1, rows, width), BF16),
            pltpu.VMEM((tp - 1, rows, width), BF16),
            pltpu.VMEM((rows, width + META), BF16),
            pltpu.VMEM((Z, rows, width + META), BF16),
            block, block, block, block,
            pltpu.VMEM((2, Z // 2, rows, width), BF16),
            pltpu.VMEM((2, Z // 2, rows, width), BF16),
            pltpu.VMEM((2 * HALF, 2 * units), BF16),
            pltpu.VMEM((width, 2 * units), BF16),
            pltpu.VMEM((width, 2 * units), BF16),
            pltpu.VMEM((2 * units, width), BF16),
            dma((3,)),
            dma((tp - 1,)), dma((tp - 1,)),
            dma((2, Z // 2)), dma((2, Z // 2)),
            dma((Z, X - 1)), dma((Z, X - 1)), dma((Z,)),
            dma((Z, X - 1)), dma((Z, X - 1)), dma((Z,)),
            dma((2, Z // 2)), dma((2, Z // 2)),
            dma((3,)), dma((3,)), dma((3,)),
        ],
        compiler_params=pltpu.CompilerParams(
            collective_id=0, has_side_effects=True, vmem_limit_bytes=58 << 20
        ),
        name="layer",
    )(
        attn_values, out_proj, residual_in, norm_gain, final_gain, router.T,
        row_order[None], routes.T, gate_weight[0], up_weight[0], down_weight[0],
    )


def solution(mesh):
    fine = Mesh(mesh.devices.reshape(X, Z, C, -1), ("x", "z", "c", "tp"))
    req = ("x", "z", "c")
    placed = (
        P(req, "tp"),
        P("tp", None),
        P((*req, "tp"), None),
        P(),
        P(),
        P(),
        P(req, None, None),
        P(req, None, None),
        P(req, None, None),
        P((*req, "tp")),
        P((*req, "tp"), None),
    )
    return jax.shard_map(
        shards, mesh=fine, in_specs=placed, out_specs=P((*req, "tp"), None), check_vma=False
    )
```
